512 devices in a mesh: dp: 8 (over z_hi, y), ctx: 64 (over z_lo, x, core).
Axes of the slice: x: 4, y: 4, z: 16 (z_hi: 2, z_lo: 8; z = z_hi * 8 + z_lo), core: 2. Of those that a mesh axis runs over, the one named last changes fastest.
Arguments:
- queries: bfloat16 [8, 8192, 1024], P('dp', 'ctx'), may hold values from -6 to 6
- keys: bfloat16 [8, 8192, 1024], P('dp', 'ctx'), may hold values from -6 to 6
- values: bfloat16 [8, 8192, 1024], P('dp', 'ctx'), may hold values from -6 to 6
- rel_bias: float32 [16, 769], replicated, may hold values from -8 to 8
- grad_out: bfloat16 [8, 8192, 1024], P('dp', 'ctx'), may hold values from -6 to 6
Outputs:
- attended: bfloat16 [8, 8192, 1024], P('dp', 'ctx')
- grad_queries: bfloat16 [8, 8192, 1024], P('dp', 'ctx')
- grad_keys: bfloat16 [8, 8192, 1024], P('dp', 'ctx')
- grad_values: bfloat16 [8, 8192, 1024], P('dp', 'ctx')
- grad_bias: float32 [16, 769], replicated
The draws below stay inside these ranges and needn't reach their ends.
All inputs are finite; a program needn't handle non-finite values.
Results may differ from the reference program's by a relative error of at most 0.024.
Values may be sent and summed in bfloat16 or wider, within the bound.
No kernel may reach another device: no remote copies, remote signals or barrier semaphores. Data moves between devices by JAX's collectives and lax.ppermute only.
A program may use at most 128 MiB of HBM per device.

```python
import math
import jax
import jax.numpy as jnp
from jax import lax

HEADS = 16
HEAD = 64
FR_DEV = 128
NB = 3
CONTEXT = 384
LENGTH = 8192
RECS = 8
WIDTH = 1024
N_CTX = 64


def draw_together(key):
    shape = (RECS, LENGTH, HEADS * HEAD)
    base = jax.random.fold_in(key, 11)
    query_key, keyed_key = jax.random.split(base, 2)
    query_draw = jnp.clip(jax.random.normal(query_key, shape, jnp.float32), -6.0, 6.0)
    keyed_draw = jnp.clip(jax.random.normal(keyed_key, shape, jnp.float32), -6.0, 6.0)
    return (query_draw, keyed_draw)


def draw_queries(key, part):
    return draw_together(key)[0].astype(jnp.bfloat16)


def draw_keys(key, part):
    return draw_together(key)[1].astype(jnp.bfloat16)


def shard_levels(stream_key, extent, pieces, low, largest):
    def one(dim, shards_of):
        heights = jax.random.uniform(jax.random.fold_in(jax.random.fold_in(stream_key, 6), dim), (shards_of,), jnp.float32, low / len(pieces), largest / len(pieces))
        return jnp.repeat(jnp.exp(heights), extent[dim] // shards_of).reshape((-1,) + (1,) * (len(extent) - dim - 1))

    loudness = one(*pieces[0])
    for cut in pieces[1:]:
        loudness = loudness * one(*cut)
    return loudness


def gaussian(key, extent, spread, reach, cuts=(), kind=jnp.bfloat16):
    values = jax.random.normal(key, extent, jnp.float32) * spread
    if len(cuts) > 0:
        values = shard_levels(key, extent, cuts, -0.22, 0.18) * values
    return jnp.clip(values, min=-reach, max=reach).astype(kind)


def setup_inputs(seed: int = 0) -> dict:
    splits = jax.random.split(jax.random.key(seed), 6)
    return {
        "queries": draw_queries(jax.random.fold_in(splits[5], 71), 0),
        "keys": draw_keys(jax.random.fold_in(splits[5], 71), 0),
        "values": gaussian(splits[2], (RECS, LENGTH, WIDTH), 1.0, 6.0, ((0, 8), (1, 64))),
        "rel_bias": gaussian(splits[3], (HEADS, 2 * CONTEXT + 1), 2.0, 8.0, (), jnp.float32),
        "grad_out": gaussian(splits[4], (RECS, LENGTH, WIDTH), 1.0, 6.0, ((0, 8), (1, 64))),
    }


excluded = -1e+30

def reference(queries, keys, values, rel_bias, grad_out):
    recs, length, width = queries.shape
    frames = FR_DEV
    blocks = N_CTX
    context = NB * frames
    span = (2 * NB + 1) * frames
    score_scale = 1.0 / math.sqrt(HEAD)
    shaped = (recs, blocks, frames, HEADS, HEAD)
    query_blocks = queries.reshape(shaped)
    grad_blocks = grad_out.reshape(shaped)
    padding = ((0, 0), (NB, NB), (0, 0), (0, 0), (0, 0))
    key_padded = jnp.pad(keys.reshape(shaped), padding)
    value_padded = jnp.pad(values.reshape(shaped), padding)
    row_index = jnp.arange(frames, dtype=jnp.int32)[:, None]
    col_index = jnp.arange(span, dtype=jnp.int32)[None, :]
    table_index = row_index - col_index + 2 * context
    inside = (table_index >= 0) & (table_index <= 2 * context)
    clipped = jnp.clip(table_index, 0, 2 * context)
    bias_table = rel_bias[:, clipped]

    def one_block(carry, block):
        key_accum, value_accum, bias_accum = carry
        query_now = lax.dynamic_index_in_dim(query_blocks, block, 1, keepdims=False).astype(jnp.float32)
        grad_now = lax.dynamic_index_in_dim(grad_blocks, block, 1, keepdims=False).astype(jnp.float32)
        key_window = lax.dynamic_slice_in_dim(key_padded, block, 2 * NB + 1, 1).reshape(recs, span, HEADS, HEAD).astype(jnp.float32)
        value_window = lax.dynamic_slice_in_dim(value_padded, block, 2 * NB + 1, 1).reshape(recs, span, HEADS, HEAD).astype(jnp.float32)
        key_place = (block - NB) * frames + col_index
        live = inside & (key_place >= 0) & (key_place < length)
        scores = jnp.einsum('rahe,rwhe->rhaw', query_now, key_window) * score_scale + bias_table[None]
        scores = jnp.where(live[None, None], scores, excluded)
        top = lax.optimization_barrier(jnp.max(scores, axis=-1))
        total = lax.optimization_barrier(jnp.sum(jnp.exp(scores - top[..., None]), axis=-1))
        log_norm = top + jnp.log(total)
        probs = jnp.exp(scores - log_norm[..., None])
        weights = lax.optimization_barrier(probs.astype(jnp.bfloat16)).astype(jnp.float32)
        output = jnp.einsum('rhaw,rwhe->rahe', weights, value_window)
        attended_now = output.astype(jnp.bfloat16)
        attended_wide = lax.optimization_barrier(attended_now).astype(jnp.float32)
        delta = jnp.einsum('rahe,rahe->rha', grad_now, attended_wide)
        dprob = jnp.einsum('rahe,rwhe->rhaw', grad_now, value_window)
        dscore = probs * (dprob - delta[..., None])
        dscore_low = lax.optimization_barrier(dscore.astype(jnp.bfloat16)).astype(jnp.float32)
        grad_query_now = (jnp.einsum('rhaw,rwhe->rahe', dscore_low, key_window) * score_scale).astype(jnp.bfloat16)
        key_terms = jnp.einsum('rhaw,rahe->rwhe', dscore_low, query_now) * score_scale
        value_terms = jnp.einsum('rhaw,rahe->rwhe', weights, grad_now)
        key_terms = lax.optimization_barrier(key_terms.astype(jnp.bfloat16)).astype(jnp.float32)
        value_terms = lax.optimization_barrier(value_terms.astype(jnp.bfloat16)).astype(jnp.float32)
        start = block * frames
        key_accum = lax.dynamic_update_slice_in_dim(key_accum, lax.dynamic_slice_in_dim(key_accum, start, span, 1) + key_terms, start, 1)
        value_accum = lax.dynamic_update_slice_in_dim(value_accum, lax.dynamic_slice_in_dim(value_accum, start, span, 1) + value_terms, start, 1)
        flat_terms = lax.optimization_barrier(jnp.sum(dscore, axis=0)).transpose(1, 2, 0).reshape(frames * span, HEADS)
        bias_accum = bias_accum + jax.ops.segment_sum(flat_terms, clipped.reshape(-1), num_segments=2 * context + 1)
        return ((key_accum, value_accum, bias_accum), (attended_now, grad_query_now))
    padded_rows = (blocks + 2 * NB) * frames
    start_carry = (jnp.zeros((recs, padded_rows, HEADS, HEAD), jnp.float32), jnp.zeros((recs, padded_rows, HEADS, HEAD), jnp.float32), jnp.zeros((2 * context + 1, HEADS), jnp.float32))
    final, stacked = lax.scan(one_block, start_carry, jnp.arange(blocks, dtype=jnp.int32))
    key_accum, value_accum, bias_accum = final
    attended = stacked[0].transpose(1, 0, 2, 3, 4).reshape(recs, length, width)
    grad_queries = stacked[1].transpose(1, 0, 2, 3, 4).reshape(recs, length, width)
    grad_keys = key_accum[:, context:context + length].astype(jnp.bfloat16).reshape(recs, length, width)
    grad_values = value_accum[:, context:context + length].astype(jnp.bfloat16).reshape(recs, length, width)
    grad_bias = bias_accum.T
    return (attended, grad_queries, grad_keys, grad_values, grad_bias)
```

```python
import math

import jax
import jax.numpy as jnp
from jax import lax
from jax.experimental import pallas as pl
from jax.experimental.pallas import tpu as pltpu
from jax.sharding import Mesh, PartitionSpec as P

HEADS = 16
HEAD = 64
FR = 128
NB = 3
CONTEXT = NB * FR
MEMB = 8
FAR = 2
CORES = 2
ROWS = MEMB * FR
PAD_ROWS = ROWS + 2 * CONTEXT
TILE = 256
WIN = TILE + 2 * CONTEXT
CH = 128
NCH = WIN // CH
DIAGS = 2 * NB + 1
LANES = 128
EXCLUDED = -1e30
SCALE = 1.0 / math.sqrt(HEAD)
F32 = jnp.float32
BF16 = jnp.bfloat16

NN = (((1,), (0,)), ((), ()))
NT = (((1,), (1,)), ((), ()))


def dot(a, b, dims):
    return lax.dot_general(a, b, dims, preferred_element_type=F32)


def attention_kernel(
    place, kv_left, kv_mid, kv_right, qd, bias_row,
    od, dkv, dkv_left, dkv_right, bias_grad,
    kv, kv_t, qd_t, table, scores, probs, dscores, key_acc, value_acc, diag_acc,
    od_t, sems,
):
    copies = [
        pltpu.make_async_copy(kv_left, kv.at[pl.ds(0, CONTEXT)], sems.at[0]),
        pltpu.make_async_copy(kv_mid, kv.at[pl.ds(CONTEXT, ROWS)], sems.at[1]),
        pltpu.make_async_copy(kv_right, kv.at[pl.ds(CONTEXT + ROWS, CONTEXT)], sems.at[2]),
    ]
    for copy in copies:
        copy.start()
    first = place[0] == 0
    last = place[0] == place[1] - 1
    key_acc[...] = jnp.zeros_like(key_acc)
    value_acc[...] = jnp.zeros_like(value_acc)
    diag_acc[...] = jnp.zeros_like(diag_acc)
    for h in range(2):
        for c in range(NCH):
            start = (-LANES * (c + 1)) % (5 * TILE)
            parts = [
                bias_row[h : h + 1, (start + LANES * n) % (5 * TILE) : (start + LANES * n) % (5 * TILE) + LANES]
                for n in range(3)
            ]
            wide = jnp.broadcast_to(jnp.concatenate(parts, axis=1), (CH, 3 * LANES))
            turned = pltpu.roll(wide, 0, 1, stride=1, stride_axis=0)
            table[h, pl.ds(c * CH, CH), :] = turned[:, LANES:]
    qd_t[...] = qd[...].T
    for copy in copies:
        copy.wait()
    kv_t[...] = kv[...].T

    lane = lax.broadcasted_iota(jnp.int32, (TILE, LANES), 1)
    small = jnp.asarray(SCALE, BF16)

    def rows(c):
        return pl.ds(c * CH, CH)

    class Part:
        def __init__(self, base, h, n):
            self.base, self.h, self.n, self.m = base, h, n % 3, n % 2
            self.o = (base // TILE) % 2
            self.head = pl.ds(h * HEAD, HEAD)
            self.own = (lane >= h * HEAD) & (lane < (h + 1) * HEAD)

        def score_start(self):
            q = qd[pl.ds(self.base, TILE), :LANES] * small
            self.q = jnp.where(self.own, q, jnp.zeros_like(q))
            self.top8 = jnp.full((8, TILE), EXCLUDED, F32)

        def score(self, c):
            at = self.base + c * CH
            s = dot(kv[pl.ds(at, CH), :LANES], self.q, NT) + table[self.h, rows(c), :]
            if c < NB or c >= NCH - NB:
                bad = (first & (at < CONTEXT)) | (last & (at >= CONTEXT + ROWS))
                s = jnp.where(bad, EXCLUDED, s)
            scores[self.n, rows(c), :] = s
            self.top8 = jnp.maximum(self.top8, jnp.max(s.reshape(CH // 8, 8, TILE), axis=0))

        def prob_start(self):
            self.top = jnp.max(self.top8, axis=0, keepdims=True)
            self.sum8 = jnp.zeros((8, TILE), F32)

        def prob(self, c):
            p = jnp.exp(scores[self.n, rows(c), :] - self.top)
            scores[self.n, rows(c), :] = p
            probs[self.n, rows(c), :] = p.astype(BF16)
            self.sum8 = self.sum8 + jnp.sum(p.reshape(CH // 8, 8, TILE), axis=0)

        def output(self):
            self.inv = 1.0 / jnp.sum(self.sum8, axis=0, keepdims=True)
            v_t = kv_t[pl.ds(LANES + self.h * HEAD, HEAD), pl.ds(self.base, WIN)]
            out_t = (dot(v_t, probs[self.n], NN) * self.inv).astype(BF16)
            od_t[self.o, self.head, :] = out_t
            d_t = qd_t[pl.ds(LANES + self.h * HEAD, HEAD), pl.ds(self.base, TILE)].astype(F32)
            self.delta = jnp.sum(out_t.astype(F32) * d_t, axis=0, keepdims=True) * self.inv
            self.d_scaled = (d_t * self.inv).astype(BF16)
            d = qd[pl.ds(self.base, TILE), LANES:]
            self.d = jnp.where(self.own, d, jnp.zeros_like(d))

        def dscore(self, c):
            at = self.base + c * CH
            dp = dot(kv[pl.ds(at, CH), LANES:], self.d, NT)
            ds = scores[self.n, rows(c), :] * (dp * self.inv - self.delta)
            dscores[self.m, rows(c), :] = ds.astype(BF16)
            for i in range(TILE // CH):
                k = i - c + DIAGS - 1
                if 0 <= k < DIAGS:
                    cols = slice((k + 1) * LANES, (k + 2) * LANES)
                    diag_acc[self.h, :, cols] += ds[:, i * CH : (i + 1) * CH]

        def value_grad(self, c):
            at, two = pl.ds(self.base + c * TILE, TILE), pl.ds(c * TILE, TILE)
            value_acc[self.head, at] += dot(self.d_scaled, probs[self.n, two, :], NT)

        def key_grad(self, c):
            at, two = pl.ds(self.base + c * TILE, TILE), pl.ds(c * TILE, TILE)
            q_t = qd_t[self.head, pl.ds(self.base, TILE)] * small
            key_acc[self.head, at] += dot(q_t, dscores[self.m, two, :], NT)

        def query_grad(self):
            k_t = kv_t[self.head, pl.ds(self.base, WIN)]
            dq_t = (dot(k_t, dscores[self.m], NN) * SCALE).astype(BF16)
            od_t[self.o, pl.ds(LANES + self.h * HEAD, HEAD), :] = dq_t

    parts = [Part(t * TILE, h, t * 2 + h) for t in range(ROWS // TILE) for h in range(2)]
    for step in range(len(parts) + 3):
        now = [parts[step - lag] if 0 <= step - lag < len(parts) else None for lag in range(4)]
        if now[0]:
            now[0].score_start()
        if now[1]:
            now[1].prob_start()
        if now[2]:
            now[2].output()
        for c in range(NCH):
            if now[0]:
                now[0].score(c)
            if now[1]:
                now[1].prob(c)
            if now[2]:
                now[2].dscore(c)
            if now[3] and c % 2:
                now[3].value_grad(c // 2)
                now[3].key_grad(c // 2)
        if now[3]:
            now[3].query_grad()
            if now[3].h == 1:
                od[pl.ds(now[3].base, TILE), :] = od_t[(now[3].base // TILE) % 2].T

    for n, acc in enumerate((key_acc, value_acc)):
        cols = slice(n * LANES, (n + 1) * LANES)
        dkv_left[:, cols] = acc[:, :CONTEXT].astype(BF16).T
        dkv[:, cols] = acc[:, CONTEXT : CONTEXT + ROWS].astype(BF16).T
        dkv_right[:, cols] = acc[:, CONTEXT + ROWS :].astype(BF16).T

    wide = (DIAGS + 1) * LANES
    part = diag_acc[...]
    size = CH
    while size > 8:
        size //= 2
        part = part[:, :size] + pltpu.roll(part[:, size:], wide - size, 2)
    sub = lax.broadcasted_iota(jnp.int32, (2, 8, wide), 1)
    for step in (4, 2, 1):
        part = jnp.where((sub & step) != 0, pltpu.roll(part, wide - step, 2), part)
    total = jnp.sum(part, axis=1)
    bias_grad[...] = total[:, LANES:]


def attention(place, kv_left, kv_mid, kv_right, qd, bias_row):
    vmem = pl.BlockSpec(memory_space=pltpu.VMEM)
    hbm = pl.BlockSpec(memory_space=pl.ANY)
    return pl.pallas_call(
        attention_kernel,
        out_shape=(
            jax.ShapeDtypeStruct((ROWS, 2 * LANES), BF16),
            jax.ShapeDtypeStruct((ROWS, 2 * LANES), BF16),
            jax.ShapeDtypeStruct((CONTEXT, 2 * LANES), BF16),
            jax.ShapeDtypeStruct((CONTEXT, 2 * LANES), BF16),
            jax.ShapeDtypeStruct((2, DIAGS * LANES), F32),
        ),
        in_specs=[pl.BlockSpec(memory_space=pltpu.SMEM), hbm, hbm, hbm, vmem, vmem],
        out_specs=(vmem,) * 5,
        scratch_shapes=[
            pltpu.VMEM((PAD_ROWS, 2 * LANES), BF16),
            pltpu.VMEM((2 * LANES, PAD_ROWS), BF16),
            pltpu.VMEM((2 * LANES, ROWS), BF16),
            pltpu.VMEM((2, WIN, TILE), F32),
            pltpu.VMEM((3, WIN, TILE), F32),
            pltpu.VMEM((3, WIN, TILE), BF16),
            pltpu.VMEM((2, WIN, TILE), BF16),
            pltpu.VMEM((LANES, PAD_ROWS), F32),
            pltpu.VMEM((LANES, PAD_ROWS), F32),
            pltpu.VMEM((2, CH, (DIAGS + 1) * LANES), F32),
            pltpu.VMEM((2, 2 * LANES, TILE), BF16),
            pltpu.SemaphoreType.DMA((3,)),
        ],
        compiler_params=pltpu.CompilerParams(vmem_limit_bytes=40 * 2**20),
        cost_estimate=pl.CostEstimate(flops=3 * 10**9, bytes_accessed=6 * 2**20, transcendentals=2 * 10**6),
        name="attention",
    )(place, kv_left, kv_mid, kv_right, qd, bias_row)


def pack_kernel(a, b, out):
    for m in range(MEMB):
        cols = slice(m * LANES, (m + 1) * LANES)
        out[m, :, :LANES] = a[0, :, cols]
        out[m, :, LANES:] = b[0, :, cols]


def pack(a, b):
    vmem = pl.BlockSpec(memory_space=pltpu.VMEM)
    return pl.pallas_call(
        pack_kernel,
        out_shape=jax.ShapeDtypeStruct((MEMB, FR, 2 * LANES), BF16),
        in_specs=[vmem, vmem],
        out_specs=vmem,
        cost_estimate=pl.CostEstimate(flops=0, bytes_accessed=2**20, transcendentals=0),
        name="pack",
    )(a, b)


def unpack_kernel(merged, *outs):
    for m in range(MEMB):
        for n, out in enumerate(outs):
            out[0, :, m * LANES : (m + 1) * LANES] = merged[m, :, n * LANES : (n + 1) * LANES]


def unpack(merged):
    vmem = pl.BlockSpec(memory_space=pltpu.VMEM)
    return pl.pallas_call(
        unpack_kernel,
        out_shape=(jax.ShapeDtypeStruct((1, FR, MEMB * LANES), BF16),) * 4,
        in_specs=[vmem],
        out_specs=(vmem,) * 4,
        cost_estimate=pl.CostEstimate(flops=0, bytes_accessed=2 * 2**20, transcendentals=0),
        name="unpack",
    )(merged)


def join_kernel(od, dkv, from_left, from_right, out):
    def add(a, b):
        return (a.astype(F32) + b.astype(F32)).astype(BF16)

    for m in range(MEMB):
        mine = pl.ds(m * FR, FR)
        out[m, :, : 2 * LANES] = od[mine]
        if m < NB:
            out[m, :, 2 * LANES :] = add(dkv[mine], from_left[mine])
        elif m >= MEMB - NB:
            out[m, :, 2 * LANES :] = add(dkv[mine], from_right[pl.ds((m - MEMB + NB) * FR, FR)])
        else:
            out[m, :, 2 * LANES :] = dkv[mine]


def join(od, dkv, from_left, from_right):
    vmem = pl.BlockSpec(memory_space=pltpu.VMEM)
    return pl.pallas_call(
        join_kernel,
        out_shape=jax.ShapeDtypeStruct((MEMB, FR, 4 * LANES), BF16),
        in_specs=[vmem] * 4,
        out_specs=vmem,
        cost_estimate=pl.CostEstimate(flops=2**18, bytes_accessed=2 * 2**20, transcendentals=0),
        name="join",
    )(od, dkv, from_left, from_right)


def to_all(x, axes):
    return lax.all_to_all(x, axes, 0, 0, tiled=True)


def shifted(x, by):
    n = lax.axis_size("grp")
    return lax.ppermute(x, "grp", [(i, i + by) for i in range(n) if 0 <= i + by < n])


def body(queries, keys, values, rel_bias, grad_out):
    groups = lax.axis_size("grp")
    kv = to_all(pack(keys, values), ("x", "core"))
    left = shifted(kv[MEMB - NB :], 1)
    right = shifted(kv[:NB], -1)
    qd = to_all(pack(queries, grad_out), ("x", "core"))
    member = lax.axis_index(("x", "core"))
    mine = lax.dynamic_slice_in_dim(rel_bias, 2 * member, 2, axis=0)
    gap = jnp.full((2, 2 * TILE - 1), EXCLUDED, F32)
    bias_row = jnp.concatenate([mine[:, 2 * CONTEXT :], gap, mine[:, : 2 * CONTEXT]], axis=1)
    place = jnp.stack([lax.axis_index("grp"), jnp.int32(groups)])
    od, dkv, dleft, dright, dbias = attention(
        place,
        left.reshape(CONTEXT, 2 * LANES),
        kv.reshape(ROWS, 2 * LANES),
        right.reshape(CONTEXT, 2 * LANES),
        qd.reshape(ROWS, 2 * LANES),
        bias_row,
    )
    from_right = shifted(dleft, -1)
    from_left = shifted(dright, 1)
    column = lax.axis_size(("far", "grp"))
    column = to_all(jnp.broadcast_to(dbias[None], (column,) + dbias.shape), ("far", "grp"))
    grads = join(od, dkv, from_left, from_right)
    grads, column = lax.optimization_barrier((grads, column))
    merged = to_all(grads, ("x", "core"))
    one = lax.psum(jnp.sum(column, axis=0), "row")
    one, merged = lax.optimization_barrier((one, merged))
    every = to_all(jnp.broadcast_to(one[None], (MEMB,) + one.shape), ("x", "core"))
    attended, grad_queries, grad_keys, grad_values = unpack(merged)
    grad_bias = every.reshape(HEADS, DIAGS * LANES)[:, : 2 * CONTEXT + 1]
    return (attended, grad_queries, grad_keys, grad_values, grad_bias)


def solution(mesh):
    dp, ctx = mesh.devices.shape
    split = (FAR, dp // FAR, ctx // MEMB, MEMB // CORES, CORES)
    fine = Mesh(mesh.devices.reshape(split), ("far", "row", "grp", "x", "core"))
    placed = P(("far", "row"), ("grp", "x", "core"), None)
    return jax.shard_map(
        body,
        mesh=fine,
        in_specs=(placed, placed, placed, P(), placed),
        out_specs=(placed, placed, placed, placed, P()),
        check_vma=False,
    )
```

```python
import math

import jax
import jax.numpy as jnp
from jax import lax
from jax.experimental import pallas as pl
from jax.experimental.pallas import tpu as pltpu
from jax.sharding import Mesh, PartitionSpec as P

HEADS = 16
HEAD = 64
FR = 128
NB = 3
CONTEXT = NB * FR
MEMB = 8
FAR = 2
CORES = 2
ROWS = MEMB * FR
PAD_ROWS = ROWS + 2 * CONTEXT
TILE = 256
WIN = TILE + 2 * CONTEXT
CH = 128
NCH = WIN // CH
DIAGS = 2 * NB + 1
LANES = 128
EXCLUDED = -1e30
SCALE = 1.0 / math.sqrt(HEAD)
F32 = jnp.float32
BF16 = jnp.bfloat16

NN = (((1,), (0,)), ((), ()))
NT = (((1,), (1,)), ((), ()))


def dot(a, b, dims):
    return lax.dot_general(a, b, dims, preferred_element_type=F32)


def attention_kernel(
    place, kv_left, kv_mid, kv_right, qd, bias_row,
    grads, dkv_left, dkv_right, bias_grad,
    kv, kv_t, qd_t, table, scores, probs, dscores, key_acc, value_acc, diag_acc,
    od_t, sems,
):
    copies = [
        pltpu.make_async_copy(kv_left, kv.at[pl.ds(0, CONTEXT)], sems.at[0]),
        pltpu.make_async_copy(kv_mid, kv.at[pl.ds(CONTEXT, ROWS)], sems.at[1]),
        pltpu.make_async_copy(kv_right, kv.at[pl.ds(CONTEXT + ROWS, CONTEXT)], sems.at[2]),
    ]
    for copy in copies:
        copy.start()
    first = place[0] == 0
    last = place[0] == place[1] - 1
    key_acc[...] = jnp.zeros_like(key_acc)
    value_acc[...] = jnp.zeros_like(value_acc)
    diag_acc[...] = jnp.zeros_like(diag_acc)
    for h in range(2):
        for c in range(NCH):
            start = (-LANES * (c + 1)) % (5 * TILE)
            parts = [
                bias_row[h : h + 1, (start + LANES * n) % (5 * TILE) : (start + LANES * n) % (5 * TILE) + LANES]
                for n in range(3)
            ]
            wide = jnp.broadcast_to(jnp.concatenate(parts, axis=1), (CH, 3 * LANES))
            turned = pltpu.roll(wide, 0, 1, stride=1, stride_axis=0)
            table[h, pl.ds(c * CH, CH), :] = turned[:, LANES:]
    qd_t[...] = qd[...].T
    for copy in copies:
        copy.wait()
    kv_t[...] = kv[...].T

    lane = lax.broadcasted_iota(jnp.int32, (TILE, LANES), 1)
    small = jnp.asarray(SCALE, BF16)

    def rows(c):
        return pl.ds(c * CH, CH)

    class Part:
        def __init__(self, base, h, n):
            self.base, self.h, self.n, self.m = base, h, n % 3, n % 2
            self.o = (base // TILE) % 2
            self.head = pl.ds(h * HEAD, HEAD)
            self.own = (lane >= h * HEAD) & (lane < (h + 1) * HEAD)

        def score_start(self):
            q = qd[pl.ds(self.base, TILE), :LANES] * small
            self.q = jnp.where(self.own, q, jnp.zeros_like(q))
            self.top8 = jnp.full((8, TILE), EXCLUDED, F32)

        def score(self, c):
            at = self.base + c * CH
            s = dot(kv[pl.ds(at, CH), :LANES], self.q, NT) + table[self.h, rows(c), :]
            if c < NB or c >= NCH - NB:
                bad = (first & (at < CONTEXT)) | (last & (at >= CONTEXT + ROWS))
                s = jnp.where(bad, EXCLUDED, s)
            scores[self.n, rows(c), :] = s
            self.top8 = jnp.maximum(self.top8, jnp.max(s.reshape(CH // 8, 8, TILE), axis=0))

        def prob_start(self):
            self.top = jnp.max(self.top8, axis=0, keepdims=True)
            self.sum8 = jnp.zeros((8, TILE), F32)

        def prob(self, c):
            p = jnp.exp(scores[self.n, rows(c), :] - self.top)
            scores[self.n, rows(c), :] = p
            probs[self.n, rows(c), :] = p.astype(BF16)
            self.sum8 = self.sum8 + jnp.sum(p.reshape(CH // 8, 8, TILE), axis=0)

        def output(self):
            self.inv = 1.0 / jnp.sum(self.sum8, axis=0, keepdims=True)
            v_t = kv_t[pl.ds(LANES + self.h * HEAD, HEAD), pl.ds(self.base, WIN)]
            out_t = (dot(v_t, probs[self.n], NN) * self.inv).astype(BF16)
            od_t[self.o, self.head, :] = out_t
            d_t = qd_t[pl.ds(LANES + self.h * HEAD, HEAD), pl.ds(self.base, TILE)].astype(F32)
            self.delta = jnp.sum(out_t.astype(F32) * d_t, axis=0, keepdims=True) * self.inv
            self.d_scaled = (d_t * self.inv).astype(BF16)
            d = qd[pl.ds(self.base, TILE), LANES:]
            self.d = jnp.where(self.own, d, jnp.zeros_like(d))

        def dscore(self, c):
            at = self.base + c * CH
            dp = dot(kv[pl.ds(at, CH), LANES:], self.d, NT)
            ds = scores[self.n, rows(c), :] * (dp * self.inv - self.delta)
            dscores[self.m, rows(c), :] = ds.astype(BF16)
            for i in range(TILE // CH):
                k = i - c + DIAGS - 1
                if 0 <= k < DIAGS:
                    cols = slice((k + 1) * LANES, (k + 2) * LANES)
                    diag_acc[self.h, :, cols] += ds[:, i * CH : (i + 1) * CH]

        def value_grad(self, c):
            at, two = pl.ds(self.base + c * TILE, TILE), pl.ds(c * TILE, TILE)
            value_acc[self.head, at] += dot(self.d_scaled, probs[self.n, two, :], NT)

        def key_grad(self, c):
            at, two = pl.ds(self.base + c * TILE, TILE), pl.ds(c * TILE, TILE)
            q_t = qd_t[self.head, pl.ds(self.base, TILE)] * small
            key_acc[self.head, at] += dot(q_t, dscores[self.m, two, :], NT)

        def query_grad(self):
            k_t = kv_t[self.head, pl.ds(self.base, WIN)]
            dq_t = (dot(k_t, dscores[self.m], NN) * SCALE).astype(BF16)
            od_t[self.o, pl.ds(LANES + self.h * HEAD, HEAD), :] = dq_t

    parts = [Part(t * TILE, h, t * 2 + h) for t in range(ROWS // TILE) for h in range(2)]
    for step in range(len(parts) + 3):
        now = [parts[step - lag] if 0 <= step - lag < len(parts) else None for lag in range(4)]
        if now[0]:
            now[0].score_start()
        if now[1]:
            now[1].prob_start()
        if now[2]:
            now[2].output()
        for c in range(NCH):
            if now[0]:
                now[0].score(c)
            if now[1]:
                now[1].prob(c)
            if now[2]:
                now[2].dscore(c)
            if now[3] and c % 2:
                now[3].value_grad(c // 2)
                now[3].key_grad(c // 2)
        if now[3]:
            now[3].query_grad()
            if now[3].h == 1:
                o, first_block = now[3].o, now[3].base // FR
                both = od_t[o].T
                for n in range(TILE // FR):
                    grads[first_block + n, 0] = both[n * FR : (n + 1) * FR]

    for n, acc in enumerate((key_acc, value_acc)):
        cols = slice(n * LANES, (n + 1) * LANES)
        dkv_left[:, cols] = acc[:, :CONTEXT].astype(BF16).T
        for m in range(MEMB):
            at = CONTEXT + m * FR
            grads[m, 1, :, cols] = acc[:, at : at + FR].astype(BF16).T
        dkv_right[:, cols] = acc[:, CONTEXT + ROWS :].astype(BF16).T

    wide = (DIAGS + 1) * LANES
    part = diag_acc[...]
    size = CH
    while size > 8:
        size //= 2
        part = part[:, :size] + pltpu.roll(part[:, size:], wide - size, 2)
    sub = lax.broadcasted_iota(jnp.int32, (2, 8, wide), 1)
    for step in (4, 2, 1):
        part = jnp.where((sub & step) != 0, pltpu.roll(part, wide - step, 2), part)
    total = jnp.sum(part, axis=1)
    total = total[:, LANES:]
    for n in range(bias_grad.shape[0]):
        bias_grad[n] = total


def attention(times, place, kv_left, kv_mid, kv_right, qd, bias_row):
    vmem = pl.BlockSpec(memory_space=pltpu.VMEM)
    hbm = pl.BlockSpec(memory_space=pl.ANY)
    return pl.pallas_call(
        attention_kernel,
        out_shape=(
            jax.ShapeDtypeStruct((MEMB, 2, FR, 2 * LANES), BF16),
            jax.ShapeDtypeStruct((CONTEXT, 2 * LANES), BF16),
            jax.ShapeDtypeStruct((CONTEXT, 2 * LANES), BF16),
            jax.ShapeDtypeStruct((times, 2, DIAGS * LANES), F32),
        ),
        in_specs=[pl.BlockSpec(memory_space=pltpu.SMEM), hbm, hbm, hbm, vmem, vmem],
        out_specs=(vmem,) * 4,
        scratch_shapes=[
            pltpu.VMEM((PAD_ROWS, 2 * LANES), BF16),
            pltpu.VMEM((2 * LANES, PAD_ROWS), BF16),
            pltpu.VMEM((2 * LANES, ROWS), BF16),
            pltpu.VMEM((2, WIN, TILE), F32),
            pltpu.VMEM((3, WIN, TILE), F32),
            pltpu.VMEM((3, WIN, TILE), BF16),
            pltpu.VMEM((2, WIN, TILE), BF16),
            pltpu.VMEM((LANES, PAD_ROWS), F32),
            pltpu.VMEM((LANES, PAD_ROWS), F32),
            pltpu.VMEM((2, CH, (DIAGS + 1) * LANES), F32),
            pltpu.VMEM((2, 2 * LANES, TILE), BF16),
            pltpu.SemaphoreType.DMA((3,)),
        ],
        compiler_params=pltpu.CompilerParams(vmem_limit_bytes=40 * 2**20),
        cost_estimate=pl.CostEstimate(flops=3 * 10**9, bytes_accessed=6 * 2**20, transcendentals=2 * 10**6),
        name="attention",
    )(place, kv_left, kv_mid, kv_right, qd, bias_row)


def pack_kernel(a, b, out):
    for m in range(MEMB):
        cols = slice(m * LANES, (m + 1) * LANES)
        out[m, :, :LANES] = a[0, :, cols]
        out[m, :, LANES:] = b[0, :, cols]


def pack(a, b):
    vmem = pl.BlockSpec(memory_space=pltpu.VMEM)
    return pl.pallas_call(
        pack_kernel,
        out_shape=jax.ShapeDtypeStruct((MEMB, FR, 2 * LANES), BF16),
        in_specs=[vmem, vmem],
        out_specs=vmem,
        cost_estimate=pl.CostEstimate(flops=0, bytes_accessed=2**20, transcendentals=0),
        name="pack",
    )(a, b)


def unpack_kernel(merged, *refs):
    outs, (blocks, sems) = refs[:4], refs[4:]
    copies = [pltpu.make_async_copy(merged.at[m], blocks.at[m], sems.at[m]) for m in range(MEMB)]
    for copy in copies:
        copy.start()
    for m in range(MEMB):
        copies[m].wait()
        for n, out in enumerate(outs):
            at = slice((n % 2) * LANES, (n % 2 + 1) * LANES)
            out[0, :, m * LANES : (m + 1) * LANES] = blocks[m, n // 2, :, at]


def unpack(merged):
    vmem = pl.BlockSpec(memory_space=pltpu.VMEM)
    return pl.pallas_call(
        unpack_kernel,
        out_shape=(jax.ShapeDtypeStruct((1, FR, MEMB * LANES), BF16),) * 4,
        in_specs=[pl.BlockSpec(memory_space=pl.ANY)],
        out_specs=(vmem,) * 4,
        scratch_shapes=[
            pltpu.VMEM((MEMB, 2, FR, 2 * LANES), BF16),
            pltpu.SemaphoreType.DMA((MEMB,)),
        ],
        cost_estimate=pl.CostEstimate(flops=0, bytes_accessed=2 * 2**20, transcendentals=0),
        name="unpack",
    )(merged)


def join_kernel(grads, from_left, from_right, out, own, far, sems):
    del grads
    halves = ((pl.ds(0, NB), from_left), (pl.ds(MEMB - NB, NB), from_right))
    loads = []
    for n, (at, halo) in enumerate(halves):
        loads.append(
            (
                pltpu.make_async_copy(out.at[at, 1], own.at[n], sems.at[2 * n]),
                pltpu.make_async_copy(halo, far.at[n], sems.at[2 * n + 1]),
            )
        )
    for pair in loads:
        for copy in pair:
            copy.start()
    stores = []
    for n, (at, halo) in enumerate(halves):
        for copy in loads[n]:
            copy.wait()
        own[n] = (own[n].astype(F32) + far[n].astype(F32)).astype(BF16)
        stores.append(pltpu.make_async_copy(own.at[n], out.at[at, 1], sems.at[4 + n]))
        stores[-1].start()
    for copy in stores:
        copy.wait()


def join(grads, from_left, from_right):
    hbm = pl.BlockSpec(memory_space=pl.ANY)
    half = pltpu.VMEM((2, NB, FR, 2 * LANES), BF16)
    return pl.pallas_call(
        join_kernel,
        out_shape=jax.ShapeDtypeStruct((MEMB, 2, FR, 2 * LANES), BF16),
        in_specs=[hbm] * 3,
        out_specs=hbm,
        scratch_shapes=[half, half, pltpu.SemaphoreType.DMA((6,))],
        input_output_aliases={0: 0},
        cost_estimate=pl.CostEstimate(flops=2**18, bytes_accessed=2**20, transcendentals=0),
        name="join",
    )(grads, from_left, from_right)


def to_all(x, axes):
    return lax.all_to_all(x, axes, 0, 0, tiled=True)


def shifted(x, by):
    n = lax.axis_size("grp")
    return lax.ppermute(x, "grp", [(i, i + by) for i in range(n) if 0 <= i + by < n])


def body(queries, keys, values, rel_bias, grad_out):
    groups = lax.axis_size("grp")
    kv = to_all(pack(keys, values), ("x", "core"))
    left = shifted(kv[MEMB - NB :], 1)
    right = shifted(kv[:NB], -1)
    qd = to_all(pack(queries, grad_out), ("x", "core"))
    member = lax.axis_index(("x", "core"))
    mine = lax.dynamic_slice_in_dim(rel_bias, 2 * member, 2, axis=0)
    gap = jnp.full((2, 2 * TILE - 1), EXCLUDED, F32)
    bias_row = jnp.concatenate([mine[:, 2 * CONTEXT :], gap, mine[:, : 2 * CONTEXT]], axis=1)
    place = jnp.stack([lax.axis_index("grp"), jnp.int32(groups)])
    column = lax.axis_size(("far", "grp"))
    grads, dleft, dright, dbias = attention(
        column,
        place,
        left.reshape(CONTEXT, 2 * LANES),
        kv.reshape(ROWS, 2 * LANES),
        right.reshape(CONTEXT, 2 * LANES),
        qd.reshape(ROWS, 2 * LANES),
        bias_row,
    )
    halo = (NB, FR, 2 * LANES)
    from_right = shifted(dleft.reshape(halo), -1)
    from_left = shifted(dright.reshape(halo), 1)
    column = to_all(dbias, ("far", "grp"))
    grads = join(grads, from_left, from_right)
    grads, column = lax.optimization_barrier((grads, column))
    merged = to_all(grads, ("x", "core"))
    one = lax.psum(jnp.sum(column, axis=0), "row")
    one, merged = lax.optimization_barrier((one, merged))
    every = to_all(jnp.broadcast_to(one[None], (MEMB,) + one.shape), ("x", "core"))
    attended, grad_queries, grad_keys, grad_values = unpack(merged)
    grad_bias = every.reshape(HEADS, DIAGS * LANES)[:, : 2 * CONTEXT + 1]
    return (attended, grad_queries, grad_keys, grad_values, grad_bias)


def solution(mesh):
    dp, ctx = mesh.devices.shape
    split = (FAR, dp // FAR, ctx // MEMB, MEMB // CORES, CORES)
    fine = Mesh(mesh.devices.reshape(split), ("far", "row", "grp", "x", "core"))
    placed = P(("far", "row"), ("grp", "x", "core"), None)
    return jax.shard_map(
        body,
        mesh=fine,
        in_specs=(placed, placed, placed, P(), placed),
        out_specs=(placed, placed, placed, placed, P()),
        check_vma=False,
    )
```

```python
import math

import jax
import jax.numpy as jnp
from jax import lax
from jax.experimental import pallas as pl
from jax.experimental.pallas import tpu as pltpu
from jax.sharding import Mesh, PartitionSpec as P

HEADS = 16
HEAD = 64
FR = 128
NB = 3
CONTEXT = NB * FR
MEMB = 8
FAR = 2
CORES = 2
ROWS = MEMB * FR
PAD_ROWS = ROWS + 2 * CONTEXT
TILE = 256
WIN = TILE + 2 * CONTEXT
CH = 128
NCH = WIN // CH
DIAGS = 2 * NB + 1
LANES = 128
EXCLUDED = -1e30
SCALE = 1.0 / math.sqrt(HEAD)
F32 = jnp.float32
BF16 = jnp.bfloat16

NN = (((1,), (0,)), ((), ()))
NT = (((1,), (1,)), ((), ()))


def dot(a, b, dims):
    return lax.dot_general(a, b, dims, preferred_element_type=F32)


def attention_kernel(
    place, kv_left, kv_mid, kv_right, qd, bias_row,
    grads, dkv_left, dkv_right, bias_grad,
    kv, kv_t, qd_t, table, scores, probs, dscores, key_acc, value_acc, diag_acc,
    od_t, sems,
):
    copies = [
        pltpu.make_async_copy(kv_left, kv.at[pl.ds(0, CONTEXT)], sems.at[0]),
        pltpu.make_async_copy(kv_mid, kv.at[pl.ds(CONTEXT, ROWS)], sems.at[1]),
        pltpu.make_async_copy(kv_right, kv.at[pl.ds(CONTEXT + ROWS, CONTEXT)], sems.at[2]),
    ]
    for copy in copies:
        copy.start()
    first = place[0] == 0
    last = place[0] == place[1] - 1
    key_acc[...] = jnp.zeros_like(key_acc)
    value_acc[...] = jnp.zeros_like(value_acc)
    diag_acc[...] = jnp.zeros_like(diag_acc)
    for h in range(2):
        dead = jnp.full((CH, LANES), EXCLUDED, F32)
        table[h, pl.ds(0, CH), LANES:] = dead
        table[h, pl.ds(DIAGS * CH, CH), :LANES] = dead
        for c in range(DIAGS):
            start = 5 * TILE - LANES * (c + 1)
            parts = [
                bias_row[h : h + 1, at : at + LANES]
                for at in (start, (start + LANES) % (5 * TILE))
            ]
            wide = jnp.broadcast_to(jnp.concatenate(parts, axis=1), (CH, 2 * LANES))
            tile = pltpu.roll(wide, 0, 1, stride=1, stride_axis=0)[:, LANES:]
            table[h, pl.ds(c * CH, CH), :LANES] = tile
            table[h, pl.ds((c + 1) * CH, CH), LANES:] = tile
    qd_t[...] = qd[...].T
    for copy in copies:
        copy.wait()
    kv_t[...] = kv[...].T

    lane = lax.broadcasted_iota(jnp.int32, (TILE, LANES), 1)
    small = jnp.asarray(SCALE, BF16)

    def rows(c):
        return pl.ds(c * CH, CH)

    class Part:
        def __init__(self, base, h, n):
            self.base, self.h, self.n, self.m = base, h, n % 3, n % 2
            self.o = (base // TILE) % 2
            self.head = pl.ds(h * HEAD, HEAD)
            self.own = (lane >= h * HEAD) & (lane < (h + 1) * HEAD)

        def score_start(self):
            q = qd[pl.ds(self.base, TILE), :LANES] * small
            self.q = jnp.where(self.own, q, jnp.zeros_like(q))
            self.top8 = jnp.full((8, TILE), EXCLUDED, F32)

        def score(self, c):
            at = self.base + c * CH
            s = dot(kv[pl.ds(at, CH), :LANES], self.q, NT) + table[self.h, rows(c), :]
            if c < NB or c >= NCH - NB:
                bad = (first & (at < CONTEXT)) | (last & (at >= CONTEXT + ROWS))
                s = jnp.where(bad, EXCLUDED, s)
            scores[self.n, rows(c), :] = s
            self.top8 = jnp.maximum(self.top8, jnp.max(s.reshape(CH // 8, 8, TILE), axis=0))

        def prob_start(self):
            self.top = jnp.max(self.top8, axis=0, keepdims=True)
            self.sum8 = jnp.zeros((8, TILE), F32)

        def prob(self, c):
            p = jnp.exp(scores[self.n, rows(c), :] - self.top)
            scores[self.n, rows(c), :] = p
            probs[self.n, rows(c), :] = p.astype(BF16)
            self.sum8 = self.sum8 + jnp.sum(p.reshape(CH // 8, 8, TILE), axis=0)

        def output(self):
            self.inv = 1.0 / jnp.sum(self.sum8, axis=0, keepdims=True)
            v_t = kv_t[pl.ds(LANES + self.h * HEAD, HEAD), pl.ds(self.base, WIN)]
            out_t = (dot(v_t, probs[self.n], NN) * self.inv).astype(BF16)
            od_t[self.o, self.head, :] = out_t
            d_t = qd_t[pl.ds(LANES + self.h * HEAD, HEAD), pl.ds(self.base, TILE)].astype(F32)
            self.delta = jnp.sum(out_t.astype(F32) * d_t, axis=0, keepdims=True) * self.inv
            self.d_scaled = (d_t * self.inv).astype(BF16)
            d = qd[pl.ds(self.base, TILE), LANES:]
            self.d = jnp.where(self.own, d, jnp.zeros_like(d))

        def dscore(self, c):
            at = self.base + c * CH
            dp = dot(kv[pl.ds(at, CH), LANES:], self.d, NT)
            ds = scores[self.n, rows(c), :] * (dp * self.inv - self.delta)
            dscores[self.m, rows(c), :] = ds.astype(BF16)
            for i in range(TILE // CH):
                k = i - c + DIAGS - 1
                if 0 <= k < DIAGS:
                    cols = slice((k + 1) * LANES, (k + 2) * LANES)
                    diag_acc[self.h, :, cols] += ds[:, i * CH : (i + 1) * CH]

        def value_grad(self, c):
            at, two = pl.ds(self.base + c * TILE, TILE), pl.ds(c * TILE, TILE)
            value_acc[self.head, at] += dot(self.d_scaled, probs[self.n, two, :], NT)

        def key_grad(self, c):
            at, two = pl.ds(self.base + c * TILE, TILE), pl.ds(c * TILE, TILE)
            q_t = qd_t[self.head, pl.ds(self.base, TILE)] * small
            key_acc[self.head, at] += dot(q_t, dscores[self.m, two, :], NT)

        def query_grad(self):
            k_t = kv_t[self.head, pl.ds(self.base, WIN)]
            dq_t = (dot(k_t, dscores[self.m], NN) * SCALE).astype(BF16)
            od_t[self.o, pl.ds(LANES + self.h * HEAD, HEAD), :] = dq_t

    parts = [Part(t * TILE, h, t * 2 + h) for t in range(ROWS // TILE) for h in range(2)]
    for step in range(len(parts) + 3):
        now = [parts[step - lag] if 0 <= step - lag < len(parts) else None for lag in range(4)]
        if now[0]:
            now[0].score_start()
        if now[1]:
            now[1].prob_start()
        if now[2]:
            now[2].output()
        for c in range(NCH):
            if now[0]:
                now[0].score(c)
            if now[1]:
                now[1].prob(c)
            if now[2]:
                now[2].dscore(c)
            if now[3] and c % 2:
                now[3].value_grad(c // 2)
                now[3].key_grad(c // 2)
        if now[3]:
            now[3].query_grad()
            if now[3].h == 1:
                o, first_block = now[3].o, now[3].base // FR
                both = od_t[o].T
                for n in range(TILE // FR):
                    grads[first_block + n, 0] = both[n * FR : (n + 1) * FR]

    for n, acc in enumerate((key_acc, value_acc)):
        cols = slice(n * LANES, (n + 1) * LANES)
        dkv_left[:, cols] = acc[:, :CONTEXT].astype(BF16).T
        for m in range(MEMB):
            at = CONTEXT + m * FR
            grads[m, 1, :, cols] = acc[:, at : at + FR].astype(BF16).T
        dkv_right[:, cols] = acc[:, CONTEXT + ROWS :].astype(BF16).T

    wide = (DIAGS + 1) * LANES
    part = diag_acc[...]
    size = CH
    while size > 8:
        size //= 2
        part = part[:, :size] + pltpu.roll(part[:, size:], wide - size, 2)
    sub = lax.broadcasted_iota(jnp.int32, (2, 8, wide), 1)
    for step in (4, 2, 1):
        part = jnp.where((sub & step) != 0, pltpu.roll(part, wide - step, 2), part)
    total = jnp.sum(part, axis=1)
    total = total[:, LANES:]
    for n in range(bias_grad.shape[0]):
        bias_grad[n] = total


def attention(times, place, kv_left, kv_mid, kv_right, qd, bias_row):
    vmem = pl.BlockSpec(memory_space=pltpu.VMEM)
    hbm = pl.BlockSpec(memory_space=pl.ANY)
    return pl.pallas_call(
        attention_kernel,
        out_shape=(
            jax.ShapeDtypeStruct((MEMB, 2, FR, 2 * LANES), BF16),
            jax.ShapeDtypeStruct((CONTEXT, 2 * LANES), BF16),
            jax.ShapeDtypeStruct((CONTEXT, 2 * LANES), BF16),
            jax.ShapeDtypeStruct((times, 2, DIAGS * LANES), F32),
        ),
        in_specs=[pl.BlockSpec(memory_space=pltpu.SMEM), hbm, hbm, hbm, vmem, vmem],
        out_specs=(vmem,) * 4,
        scratch_shapes=[
            pltpu.VMEM((PAD_ROWS, 2 * LANES), BF16),
            pltpu.VMEM((2 * LANES, PAD_ROWS), BF16),
            pltpu.VMEM((2 * LANES, ROWS), BF16),
            pltpu.VMEM((2, WIN, TILE), F32),
            pltpu.VMEM((3, WIN, TILE), F32),
            pltpu.VMEM((3, WIN, TILE), BF16),
            pltpu.VMEM((2, WIN, TILE), BF16),
            pltpu.VMEM((LANES, PAD_ROWS), F32),
            pltpu.VMEM((LANES, PAD_ROWS), F32),
            pltpu.VMEM((2, CH, (DIAGS + 1) * LANES), F32),
            pltpu.VMEM((2, 2 * LANES, TILE), BF16),
            pltpu.SemaphoreType.DMA((3,)),
        ],
        compiler_params=pltpu.CompilerParams(vmem_limit_bytes=40 * 2**20),
        cost_estimate=pl.CostEstimate(flops=3 * 10**9, bytes_accessed=6 * 2**20, transcendentals=2 * 10**6),
        name="attention",
    )(place, kv_left, kv_mid, kv_right, qd, bias_row)


def pack_kernel(a, b, out):
    for m in range(MEMB):
        cols = slice(m * LANES, (m + 1) * LANES)
        out[m, :, :LANES] = a[0, :, cols]
        out[m, :, LANES:] = b[0, :, cols]


def pack(a, b):
    vmem = pl.BlockSpec(memory_space=pltpu.VMEM)
    return pl.pallas_call(
        pack_kernel,
        out_shape=jax.ShapeDtypeStruct((MEMB, FR, 2 * LANES), BF16),
        in_specs=[vmem, vmem],
        out_specs=vmem,
        cost_estimate=pl.CostEstimate(flops=0, bytes_accessed=2**20, transcendentals=0),
        name="pack",
    )(a, b)


def unpack_kernel(merged, *refs):
    outs, (blocks, sems) = refs[:4], refs[4:]
    copies = [pltpu.make_async_copy(merged.at[m], blocks.at[m], sems.at[m]) for m in range(MEMB)]
    for copy in copies:
        copy.start()
    for m in range(MEMB):
        copies[m].wait()
        for n, out in enumerate(outs):
            at = slice((n % 2) * LANES, (n % 2 + 1) * LANES)
            out[0, :, m * LANES : (m + 1) * LANES] = blocks[m, n // 2, :, at]


def unpack(merged):
    vmem = pl.BlockSpec(memory_space=pltpu.VMEM)
    return pl.pallas_call(
        unpack_kernel,
        out_shape=(jax.ShapeDtypeStruct((1, FR, MEMB * LANES), BF16),) * 4,
        in_specs=[pl.BlockSpec(memory_space=pl.ANY)],
        out_specs=(vmem,) * 4,
        scratch_shapes=[
            pltpu.VMEM((MEMB, 2, FR, 2 * LANES), BF16),
            pltpu.SemaphoreType.DMA((MEMB,)),
        ],
        cost_estimate=pl.CostEstimate(flops=0, bytes_accessed=2 * 2**20, transcendentals=0),
        name="unpack",
    )(merged)


def join_kernel(grads, from_left, from_right, out, own, far, sems):
    del grads
    halves = ((pl.ds(0, NB), from_left), (pl.ds(MEMB - NB, NB), from_right))
    loads = []
    for n, (at, halo) in enumerate(halves):
        loads.append(
            (
                pltpu.make_async_copy(out.at[at, 1], own.at[n], sems.at[2 * n]),
                pltpu.make_async_copy(halo, far.at[n], sems.at[2 * n + 1]),
            )
        )
    for pair in loads:
        for copy in pair:
            copy.start()
    stores = []
    for n, (at, halo) in enumerate(halves):
        for copy in loads[n]:
            copy.wait()
        own[n] = (own[n].astype(F32) + far[n].astype(F32)).astype(BF16)
        stores.append(pltpu.make_async_copy(own.at[n], out.at[at, 1], sems.at[4 + n]))
        stores[-1].start()
    for copy in stores:
        copy.wait()


def join(grads, from_left, from_right):
    hbm = pl.BlockSpec(memory_space=pl.ANY)
    half = pltpu.VMEM((2, NB, FR, 2 * LANES), BF16)
    return pl.pallas_call(
        join_kernel,
        out_shape=jax.ShapeDtypeStruct((MEMB, 2, FR, 2 * LANES), BF16),
        in_specs=[hbm] * 3,
        out_specs=hbm,
        scratch_shapes=[half, half, pltpu.SemaphoreType.DMA((6,))],
        input_output_aliases={0: 0},
        cost_estimate=pl.CostEstimate(flops=2**18, bytes_accessed=2**20, transcendentals=0),
        name="join",
    )(grads, from_left, from_right)


def to_all(x, axes):
    return lax.all_to_all(x, axes, 0, 0, tiled=True)


def shifted(x, by):
    n = lax.axis_size("grp")
    return lax.ppermute(x, "grp", [(i, i + by) for i in range(n) if 0 <= i + by < n])


def body(queries, keys, values, rel_bias, grad_out):
    groups = lax.axis_size("grp")
    kv = to_all(pack(keys, values), ("x", "core"))
    left = shifted(kv[MEMB - NB :], 1)
    right = shifted(kv[:NB], -1)
    qd = to_all(pack(queries, grad_out), ("x", "core"))
    member = lax.axis_index(("x", "core"))
    mine = lax.dynamic_slice_in_dim(rel_bias, 2 * member, 2, axis=0)
    gap = jnp.full((2, 2 * TILE - 1), EXCLUDED, F32)
    bias_row = jnp.concatenate([mine[:, 2 * CONTEXT :], gap, mine[:, : 2 * CONTEXT]], axis=1)
    place = jnp.stack([lax.axis_index("grp"), jnp.int32(groups)])
    column = lax.axis_size(("far", "grp"))
    grads, dleft, dright, dbias = attention(
        column,
        place,
        left.reshape(CONTEXT, 2 * LANES),
        kv.reshape(ROWS, 2 * LANES),
        right.reshape(CONTEXT, 2 * LANES),
        qd.reshape(ROWS, 2 * LANES),
        bias_row,
    )
    halo = (NB, FR, 2 * LANES)
    from_right = shifted(dleft.reshape(halo), -1)
    from_left = shifted(dright.reshape(halo), 1)
    column = to_all(dbias, ("far", "grp"))
    grads = join(grads, from_left, from_right)
    grads, column = lax.optimization_barrier((grads, column))
    merged = to_all(grads, ("x", "core"))
    one = lax.psum(jnp.sum(column, axis=0), "row")
    one, merged = lax.optimization_barrier((one, merged))
    every = to_all(jnp.broadcast_to(one[None], (MEMB,) + one.shape), ("x", "core"))
    attended, grad_queries, grad_keys, grad_values = unpack(merged)
    grad_bias = every.reshape(HEADS, DIAGS * LANES)[:, : 2 * CONTEXT + 1]
    return (attended, grad_queries, grad_keys, grad_values, grad_bias)


def solution(mesh):
    dp, ctx = mesh.devices.shape
    split = (FAR, dp // FAR, ctx // MEMB, MEMB // CORES, CORES)
    fine = Mesh(mesh.devices.reshape(split), ("far", "row", "grp", "x", "core"))
    placed = P(("far", "row"), ("grp", "x", "core"), None)
    return jax.shard_map(
        body,
        mesh=fine,
        in_specs=(placed, placed, placed, P(), placed),
        out_specs=(placed, placed, placed, placed, P()),
        check_vma=False,
    )
```
